256 devices in a mesh: egrp: 16 (over z_lo, x), inner: 16 (over z_hi, y, core).
Axes of the slice: x: 4, y: 4, z: 8 (z_hi: 2, z_lo: 4; z = z_hi * 4 + z_lo), core: 2. Of those that a mesh axis runs over, the one named last changes fastest.
Arguments:
- retarded: float32 [256, 2, 16, 128, 128], P(('egrp', 'inner')), may hold values from -0.31819806 to 0.31819806
- injection: float32 [256, 2, 16, 128, 128], P(('egrp', 'inner')), may hold values from -6 to 6
- coupling_matrices: float32 [2, 128, 128], replicated, may hold values from -0.5 to 0.5
- phonon_weight: float32 [2, 2], replicated, may hold values from 0.3 to 1
- phonon_shift: int32 [2], replicated, may hold values from 1 to 8, as said below
- slice_neighbour: int32 [16], replicated, may hold values from 0 to 15, as said below
Outputs:
- lesser_green: float32 [256, 2, 16, 128, 128], P(('egrp', 'inner'))
- phonon_sigma: float32 [256, 2, 16, 128, 128], P(('egrp', 'inner'))
The draws below stay inside these ranges and needn't reach their ends.
Inputs may be any that keep to these rules, and one draw needn't show every extreme that they name: `phonon_shift`: every entry is at least 1, and one entry equals 8. `slice_neighbour`: entry s is s - 1 or s + 1.
All inputs are finite; a program needn't handle non-finite values.
Results may differ from the reference program's by a relative error of at most 0.00015.
Values sent between devices are 32-bit elements; how exact they have to be, the bound alone decides.
No kernel may reach another device: no remote copies, remote signals or barrier semaphores. Data moves between devices by JAX's collectives and lax.ppermute only.
A program may use at most 64 MiB of HBM per device.

```python
import math
import jax
import jax.numpy as jnp
from jax import lax

NO = 128
NS = 16
NMODE = 2
MAXSHIFT = 8
ITERS = 2
NE = 256


def draw_phonon_shift(key, part):
    first_key, second_key = jax.random.split(jax.random.fold_in(key, 11))
    chosen = jax.random.randint(first_key, (), 0, NMODE)
    others = jax.random.randint(second_key, (NMODE,), 1, MAXSHIFT + 1)
    return jnp.where(jnp.arange(NMODE) == chosen, MAXSHIFT, others).astype(jnp.int32)


def draw_slice_neighbour(key, part):
    leftward = jax.random.randint(jax.random.fold_in(key, 23), (NS,), 0, 2)
    slices = jnp.arange(NS)
    picked = jnp.where(leftward == 1, slices - 1, slices + 1)
    picked = jnp.where(slices == 0, 1, picked)
    picked = jnp.where(slices == NS - 1, NS - 2, picked)
    return picked.astype(jnp.int32)


def levels(stream_key, dims, cuts, least, high):
    loudness = 1.0
    for dim, shards_of in cuts:
        heights = jax.random.uniform(jax.random.fold_in(jax.random.fold_in(stream_key, 6), dim), (shards_of,), jnp.float32, least / len(cuts), high / len(cuts))
        loudness = loudness * jnp.repeat(jnp.exp(heights), dims[dim] // shards_of).reshape((-1,) + (1,) * (len(dims) - 1 - dim))
    return loudness


def scatter_about(key, shape, spread, bound, cuts=(), dtype=jnp.bfloat16):
    array = spread * jax.random.normal(key, shape, jnp.float32)
    if cuts:
        array = array * levels(key, shape, cuts, -0.22, 0.18)
    return jnp.clip(array, -bound, bound).astype(dtype)


def setup_inputs(seed: int = 0) -> dict:
    key_list = jax.random.split(jax.random.key(seed), 7)
    retarded = scatter_about(key_list[0], (NE, 2, NS, NO, NO), (0.6 * NO ** -0.5), 0.31819806, ((0, 256),), jnp.float32)
    injection = scatter_about(key_list[1], (NE, 2, NS, NO, NO), 1.0, 6.0, ((0, 256),), jnp.float32)
    coupling_matrices = scatter_about(key_list[2], (NMODE, NO, NO), NO ** -0.5, 0.5, (), jnp.float32)
    phonon_weight = jnp.clip(jnp.exp(jax.random.uniform(key_list[3], (NMODE, 2), jnp.float32, math.log(0.3), math.log(1.0))), 0.3, 1.0)
    phonon_shift = draw_phonon_shift(jax.random.fold_in(key_list[6], 71), 0)
    slice_neighbour = draw_slice_neighbour(jax.random.fold_in(key_list[6], 71), 0)
    return {"retarded": retarded, "injection": injection, "coupling_matrices": coupling_matrices, "phonon_weight": phonon_weight, "phonon_shift": phonon_shift, "slice_neighbour": slice_neighbour}


HIGHEST = lax.Precision.HIGHEST


def product(first, second):
    return jnp.einsum('eij,ejk->eik', first, second, precision=HIGHEST)


def product_adjoint(first, second):
    return jnp.einsum('eij,ekj->eik', first, second, precision=HIGHEST)


def sandwich(green_ret, source):
    real_green, imag_green = green_ret[:, 0], green_ret[:, 1]
    real_source, imag_source = source[:, 0], source[:, 1]
    real_inner = product(real_green, real_source) - product(imag_green, imag_source)
    imag_inner = product(real_green, imag_source) + product(imag_green, real_source)
    real_outer = product_adjoint(real_inner, real_green) + product_adjoint(imag_inner, imag_green)
    imag_outer = product_adjoint(imag_inner, real_green) - product_adjoint(real_inner, imag_green)
    return jnp.stack([real_outer, imag_outer], axis=1)


def couple(mixed_green, coupling_matrices, phonon_weight, phonon_shift):
    energies = mixed_green.shape[0]
    padded = jnp.pad(mixed_green, ((MAXSHIFT, MAXSHIFT), (0, 0), (0, 0), (0, 0)))
    accumulated = jnp.zeros_like(mixed_green)
    for phonon in range(NMODE):
        shifted_up = lax.dynamic_slice_in_dim(padded, (MAXSHIFT + phonon_shift[phonon]).astype(jnp.int32), energies, 0)
        shifted_down = lax.dynamic_slice_in_dim(padded, (MAXSHIFT - phonon_shift[phonon]).astype(jnp.int32), energies, 0)
        summed = phonon_weight[phonon, 0] * shifted_up + phonon_weight[phonon, 1] * shifted_down
        matrix = coupling_matrices[phonon]
        halfway = jnp.einsum('ij,ecjk->ecik', matrix, summed, precision=HIGHEST)
        accumulated = accumulated + jnp.einsum('ecik,lk->ecil', halfway, matrix, precision=HIGHEST)
    return accumulated


def reference(retarded, injection, coupling_matrices, phonon_weight, phonon_shift, slice_neighbour):
    green_slices = jnp.moveaxis(retarded, 2, 0)
    inject_slices = jnp.moveaxis(injection, 2, 0)
    phonon_sigma = jnp.zeros_like(green_slices)
    lesser = jnp.zeros_like(green_slices)
    for iteration in range(ITERS):
        lesser = lax.map(lambda operands: sandwich(operands[0], operands[1] + operands[2]),
                         (green_slices, inject_slices, phonon_sigma))
        mixed_green = lesser + 0.5 * jnp.take(lesser, slice_neighbour, axis=0)
        phonon_sigma = lax.map(lambda blocks: couple(blocks, coupling_matrices, phonon_weight, phonon_shift), mixed_green)
    return jnp.moveaxis(lesser, 0, 2), jnp.moveaxis(phonon_sigma, 0, 2)
```

```python
import functools

import jax
import jax.numpy as jnp
from jax import lax
from jax.experimental import pallas as pl
from jax.experimental.pallas import tpu as pltpu
from jax.sharding import PartitionSpec as P

F32 = jnp.float32
BF16 = jnp.bfloat16
CHUNK = 4
BOTH = ("egrp", "inner")


def split(x):
    high = x.astype(BF16)
    return high, (x - high.astype(F32)).astype(BF16)


def dot(a, b):
    return lax.dot_general(a, b, (((1,), (0,)), ((), ())), preferred_element_type=F32)


def dot_t(a, b):
    return lax.dot_general(a, b, (((1,), (1,)), ((), ())), preferred_element_type=F32)


def dot3(a, b, product):
    a_high, a_low = split(a)
    b_high, b_low = split(b)
    return product(a_high, b_high) + (product(a_high, b_low) + product(a_low, b_high))


def sandwich(real, imag, source_real, source_imag):
    row = jnp.concatenate([real, imag], axis=1)
    source = jnp.concatenate(
        [
            jnp.concatenate([source_real, source_imag], axis=1),
            jnp.concatenate([-source_imag, source_real], axis=1),
        ],
        axis=0,
    )
    inner = dot3(row, source, dot)
    adjoint = jnp.concatenate([row, jnp.concatenate([-imag, real], axis=1)], axis=0)
    outer = dot3(inner, adjoint, dot_t)
    size = real.shape[0]
    return outer[:, :size], outer[:, size:]


def first_kernel(half_ref, near_ref, green_ref, inject_ref, away0_ref, away1_ref, home_ref, held):
    step = pl.program_id(0)
    slices = held.shape[0]
    group = slices // 2
    offset = group * (1 - half_ref[0])
    place = lax.rem(offset + step, slices)
    real, imag = sandwich(
        green_ref[0, 0, 0], green_ref[0, 1, 0], inject_ref[0, 0, 0], inject_ref[0, 1, 0]
    )
    held[place, 0] = real
    held[place, 1] = imag

    @pl.when(step == slices - 1)
    def _():
        for index in range(slices):
            at = lax.rem(offset + index, slices)
            near = near_ref[at]
            for part in range(2):
                value = held[at, part] + 0.5 * held[near, part]
                if index < CHUNK:
                    away0_ref[index, part] = value
                elif index < group:
                    away1_ref[index - CHUNK, part] = value
                else:
                    chunk, inside = divmod(index - group, CHUNK)
                    home_ref[2 * inside + part, chunk] = value


def first(half, near, green, inject):
    _, _, slices, size, _ = green.shape
    block = pl.BlockSpec(
        (1, 2, 1, size, size),
        lambda i, h, n: (0, 0, lax.rem(slices // 2 * (1 - h[0]) + i, slices), 0, 0),
    )
    away = jax.ShapeDtypeStruct((CHUNK, 2, size, size), F32)
    home = jax.ShapeDtypeStruct((2 * CHUNK, 2, size, size), F32)
    whole = lambda i, h, n: (0, 0, 0, 0)
    return pl.pallas_call(
        first_kernel,
        out_shape=(away, away, home),
        grid_spec=pltpu.PrefetchScalarGridSpec(
            num_scalar_prefetch=2,
            grid=(slices,),
            in_specs=[block, block],
            out_specs=[
                pl.BlockSpec(away.shape, whole),
                pl.BlockSpec(away.shape, whole),
                pl.BlockSpec(home.shape, whole),
            ],
            scratch_shapes=[pltpu.VMEM((slices, 2, size, size), F32)],
        ),
        cost_estimate=pl.CostEstimate(flops=4_000_000_000, bytes_accessed=6 << 20, transcendentals=0),
        name="first",
    )(half, near, green, inject)


def second_kernel(start_ref, green_ref, inject_ref, sigma_ref, into_ref, lesser_ref, unit_ref):
    del into_ref
    real, imag = sandwich(
        green_ref[0, 0, 0],
        green_ref[0, 1, 0],
        inject_ref[0, 0, 0] + sigma_ref[0, 0],
        inject_ref[0, 1, 0] + sigma_ref[0, 1],
    )
    lesser_ref[0, 0, 0] = real
    lesser_ref[0, 1, 0] = imag
    unit_ref[0, 0] = real
    unit_ref[0, 1] = imag


def second(start, green, inject, sigma, into):
    _, _, slices, size, _ = green.shape
    block = pl.BlockSpec((1, 2, 1, size, size), lambda i, s: (0, 0, s[0] + i, 0, 0))
    unit = pl.BlockSpec((1, 2, size, size), lambda i, s: (i, 0, 0, 0))
    return pl.pallas_call(
        second_kernel,
        out_shape=(
            jax.ShapeDtypeStruct(green.shape, F32),
            jax.ShapeDtypeStruct((CHUNK, 2, size, size), F32),
        ),
        grid_spec=pltpu.PrefetchScalarGridSpec(
            num_scalar_prefetch=1,
            grid=(CHUNK,),
            in_specs=[block, block, unit, pl.BlockSpec(memory_space=pl.ANY)],
            out_specs=[block, unit],
        ),
        input_output_aliases={4: 0},
        cost_estimate=pl.CostEstimate(flops=1_000_000_000, bytes_accessed=2 << 20, transcendentals=0),
        name="second",
    )(start, green, inject, sigma, into)


def couple_kernel(half_ref, shift_ref, weight_ref, matrix_ref, low_ref, mid_ref, high_ref, out_ref, window):
    count = mid_ref.shape[0]
    size = mid_ref.shape[-1]
    flip = half_ref[0]
    for index in range(count):
        window[2 * count * flip + index] = low_ref[index].reshape(size, size)
        window[count + index] = mid_ref[index].reshape(size, size)
        window[2 * count * (1 - flip) + index] = high_ref[index].reshape(size, size)
    right = []
    left_high, left_low = [], []
    for mode in range(2):
        shift = shift_ref[mode]
        summed = jnp.concatenate(
            [
                weight_ref[mode, 0] * window[count + t + shift]
                + weight_ref[mode, 1] * window[count + t - shift]
                for t in range(count)
            ],
            axis=0,
        )
        matrix_high, matrix_low = split(matrix_ref[mode])
        left_high.append(matrix_high)
        left_low.append(matrix_low)
        high, low = split(summed)
        right.append(
            dot_t(
                jnp.concatenate([high, low], axis=1),
                jnp.concatenate([matrix_high, matrix_high], axis=1),
            )
            + dot_t(high, matrix_low)
        )
    both_high = jnp.concatenate(left_high, axis=1)
    both_low = jnp.concatenate(left_low, axis=1)
    for t in range(0, count, 2):
        stacked = jnp.concatenate(
            [
                jnp.concatenate([right[m][(t + i) * size : (t + i + 1) * size] for i in range(2)], axis=1)
                for m in range(2)
            ],
            axis=0,
        )
        high, low = split(stacked)
        out = dot(both_high, high) + (dot(both_low, high) + dot(both_high, low))
        for i in range(2):
            out_ref[t + i] = out[:, i * size : (i + 1) * size]


def couple(half, shift, weight, matrices, low, mid, high):
    size = matrices.shape[-1]
    count = mid[0].shape[0]
    smem = pl.BlockSpec(memory_space=pltpu.SMEM)

    def spec(array, chunk):
        if chunk is None:
            return pl.BlockSpec(array.shape, lambda i: (0,) * array.ndim)
        return pl.BlockSpec((count, 1, size, size), lambda i: (0, chunk, 0, 0))

    return pl.pallas_call(
        couple_kernel,
        out_shape=jax.ShapeDtypeStruct((count, size, size), F32),
        grid=(1,),
        in_specs=[
            smem,
            smem,
            smem,
            pl.BlockSpec(matrices.shape, lambda i: (0, 0, 0)),
            spec(*low),
            spec(*mid),
            spec(*high),
        ],
        out_specs=pl.BlockSpec((count, size, size), lambda i: (0, 0, 0)),
        scratch_shapes=[pltpu.VMEM((3 * count, size, size), F32)],
        cost_estimate=pl.CostEstimate(flops=1_000_000_000, bytes_accessed=2 << 20, transcendentals=0),
        name="couple",
    )(half, shift, weight, matrices, low[0], mid[0], high[0])


def last_kernel(half_ref, near_ref, away0_ref, away1_ref, home0_ref, home1_ref, out_ref, held):
    step = pl.program_id(0)
    slices = held.shape[0]
    offset = slices // 2 * (1 - half_ref[0])

    @pl.when(step == 0)
    def _():
        for chunk, ref in enumerate((away0_ref, away1_ref, home0_ref, home1_ref)):
            for index in range(CHUNK):
                at = lax.rem(offset + chunk * CHUNK + index, slices)
                held[at] = ref[index]

    near = near_ref[step]
    for part in range(2):
        out_ref[0, part, 0] = held[step, part] + 0.5 * held[near, part]


def last(half, near, pieces, shape):
    _, _, slices, size, _ = shape
    whole = pl.BlockSpec((CHUNK, 2, size, size), lambda i, h, n: (0, 0, 0, 0))
    return pl.pallas_call(
        last_kernel,
        out_shape=jax.ShapeDtypeStruct(shape, F32),
        grid_spec=pltpu.PrefetchScalarGridSpec(
            num_scalar_prefetch=2,
            grid=(slices,),
            in_specs=[whole] * 4,
            out_specs=pl.BlockSpec((1, 2, 1, size, size), lambda i, h, n: (0, 0, i, 0, 0)),
            scratch_shapes=[pltpu.VMEM((slices, 2, size, size), F32)],
        ),
        name="last",
    )(half, near, *pieces)


def local(windows, retarded, injection, coupling_matrices, phonon_weight, phonon_shift, slice_neighbour):
    size = retarded.shape[-1]
    position = lax.axis_index("inner")
    half = (position // 8).astype(jnp.int32).reshape(1)
    groups = [list(range(8)), list(range(8, 16))]
    across = [(i, (i + 8) % 16) for i in range(16)]

    def neighbours(sign):
        pairs = []
        for w in range(windows):
            for i in range(16):
                to = w + sign * (1 if i >= 8 else -1)
                if 0 <= to < windows:
                    pairs.append((w * 16 + i, to * 16 + i))
        return pairs

    home_pairs, away_pairs = neighbours(1), neighbours(-1)

    def exchange(x):
        return lax.ppermute(x, "inner", across)

    def spread(x):
        return lax.all_to_all(x, "inner", 0, 0, axis_index_groups=groups, tiled=True)

    def halo(x, pairs):
        return lax.ppermute(x, BOTH, pairs)

    def units(x):
        return x.reshape(2 * CHUNK, size, size)

    def slabs(x):
        return x.reshape(CHUNK, 2, size, size)

    run = functools.partial(couple, half, phonon_shift, phonon_weight, coupling_matrices)

    away0, away1, home = first(half, slice_neighbour, retarded, injection)
    got = [exchange(away0), exchange(away1)]
    home = spread(home)
    home_halo = halo(home, home_pairs)
    homes = [(home, 0), (home, 1)]
    home_halos = [(home_halo, 0), (home_halo, 1)]
    lesser = jnp.zeros_like(injection)
    for iteration in range(2):
        backs, heres = [], []
        for chunk in range(2):
            away = spread(units(got[chunk]))
            away_halo = halo(away, away_pairs)
            back = run(homes[chunk], (away, None), home_halos[chunk])
            backs.append(exchange(slabs(spread(back))))
            here = run((away_halo, None), homes[chunk], (away, None))
            heres.append(slabs(spread(here)))
        if iteration == 0:
            got, homes, home_halos = [], [], []
            for chunk in range(2):
                lesser, unit = second(8 * half + CHUNK * chunk, retarded, injection, heres[chunk], lesser)
                unit = spread(units(unit))
                homes.append((unit, None))
                home_halos.append((halo(unit, home_pairs), None))
                lesser, unit = second(8 * (1 - half) + CHUNK * chunk, retarded, injection, backs[chunk], lesser)
                got.append(exchange(unit))
    sigma = last(half, slice_neighbour, backs + heres, injection.shape)
    return lesser, sigma


def solution(mesh):
    blocks = P(BOTH, None, None, None, None)
    return jax.shard_map(
        functools.partial(local, mesh.shape["egrp"]),
        mesh=mesh,
        in_specs=(blocks, blocks, P(), P(), P(), P()),
        out_specs=(blocks, blocks),
        check_vma=False,
    )
```

```python
import functools

import jax
import jax.numpy as jnp
from jax import lax
from jax.experimental import pallas as pl
from jax.experimental.pallas import tpu as pltpu
from jax.sharding import PartitionSpec as P


F32 = jnp.float32
BF16 = jnp.bfloat16
CHUNK = 4
BOTH = ("egrp", "inner")
SMEM = pl.BlockSpec(memory_space=pltpu.SMEM)
VMEM = pl.BlockSpec(memory_space=pltpu.VMEM)
PARAMS = pltpu.CompilerParams(vmem_limit_bytes=16 << 20)
HBM = pl.BlockSpec(memory_space=pltpu.HBM)


def far(x):
    return pltpu.with_memory_space_constraint(x, pltpu.HBM)


def near_core(x):
    return pltpu.with_memory_space_constraint(x, pltpu.VMEM)


def split(x):
    high = x.astype(BF16)
    return high, (x - high.astype(F32)).astype(BF16)


def dot(a, b):
    return lax.dot_general(a, b, (((1,), (0,)), ((), ())), preferred_element_type=F32)


def dot_t(a, b):
    return lax.dot_general(a, b, (((1,), (1,)), ((), ())), preferred_element_type=F32)


def dot3(a, b, product):
    a_high, a_low = split(a)
    b_high, b_low = split(b)
    return product(a_high, b_high) + (product(a_high, b_low) + product(a_low, b_high))


def sandwich(real, imag, source_real, source_imag):
    row = jnp.concatenate([real, imag], axis=1)
    source = jnp.concatenate(
        [
            jnp.concatenate([source_real, source_imag], axis=1),
            jnp.concatenate([-source_imag, source_real], axis=1),
        ],
        axis=0,
    )
    inner = dot3(row, source, dot)
    adjoint = jnp.concatenate([row, jnp.concatenate([-imag, real], axis=1)], axis=0)
    outer = dot3(inner, adjoint, dot_t)
    size = real.shape[0]
    return outer[:, :size], outer[:, size:]


def first_kernel(meta_ref, near_ref, green_ref, inject_ref, *refs):
    outs, (green, inject, held, sems) = refs[:-4], refs[-4:]
    slices = held.shape[0]
    group = slices // 2
    half = meta_ref[0]

    def fetch(k):
        at = lax.rem(group * (1 - half) + k, slices)
        return (
            pltpu.make_async_copy(green_ref.at[0, :, at], green.at[at], sems.at[0, k]),
            pltpu.make_async_copy(inject_ref.at[0, :, at], inject.at[at], sems.at[1, k]),
        )

    for k in range(slices):
        for copy in fetch(k):
            copy.start()

    def work(step, carry):
        for i in range(CHUNK):
            k = step * CHUNK + i
            at = lax.rem(group * (1 - half) + k, slices)
            for copy in fetch(k):
                copy.wait()
        for i in range(CHUNK):
            at = lax.rem(group * (1 - half) + step * CHUNK + i, slices)
            real, imag = sandwich(green[at, 0], green[at, 1], inject[at, 0], inject[at, 1])
            held[at, 0] = real
            held[at, 1] = imag
        return carry

    lax.fori_loop(0, slices // CHUNK, work, 0)

    def mixed(at, part):
        return held[at, part] + 0.5 * held[near_ref[at], part]

    for index in range(slices):
        at = lax.rem(group * (1 - half) + index, slices)
        chunk, j = divmod(index % group, CHUNK)
        for part in range(2):
            value = mixed(at, part)
            there = index < group
            if chunk:
                outs[2][2 * j + part, int(there)] = value
            else:
                outs[0 if there else 1][2 * j + part] = value


def first(meta, near, green, inject):
    _, _, slices, size, _ = green.shape
    away = pltpu.VMEM((2 * CHUNK, size, size), F32)
    both = pltpu.VMEM((2 * CHUNK, 2, size, size), F32)
    store = pltpu.VMEM((slices, 2, size, size), F32)
    return pl.pallas_call(
        first_kernel,
        out_shape=(away, away, both),
        in_specs=[SMEM, SMEM, HBM, HBM],
        out_specs=(VMEM,) * 3,
        scratch_shapes=[store, store, store, pltpu.SemaphoreType.DMA((2, slices))],
        cost_estimate=pl.CostEstimate(flops=4_000_000_000, bytes_accessed=6 << 20, transcendentals=0),
        compiler_params=PARAMS,
        name="first",
    )(meta, near, far(green), far(inject))


def second_kernel(chunks, start_ref, green_ref, inject_ref, sigma_ref, out_ref, green, inject, sems):
    count = chunks * CHUNK
    parts = range(0, count, CHUNK)

    def fetch(i):
        at = start_ref[i // CHUNK] + i % CHUNK
        return (
            pltpu.make_async_copy(green_ref.at[0, :, at], green.at[i], sems.at[0, i]),
            pltpu.make_async_copy(inject_ref.at[0, :, at], inject.at[i], sems.at[1, i]),
        )

    def unit(ref, i, part):
        row = 2 * (i % CHUNK) + part
        return ref.at[row, i // CHUNK] if chunks > 1 else ref.at[row]

    for i in range(count):
        for copy in fetch(i):
            copy.start()
    for first_of in parts:
        for i in range(first_of, first_of + CHUNK):
            for copy in fetch(i):
                copy.wait()
        for i in range(first_of, first_of + CHUNK):
            result = sandwich(
                green[i, 0],
                green[i, 1],
                inject[i, 0] + unit(sigma_ref, i, 0)[...],
                inject[i, 1] + unit(sigma_ref, i, 1)[...],
            )
            for part in range(2):
                unit(out_ref, i, part)[...] = result[part]


def second(start, green, inject, sigma):
    chunks = sigma.ndim - 2
    size = green.shape[-1]
    held = pltpu.VMEM((chunks * CHUNK, 2, size, size), F32)
    return pl.pallas_call(
        functools.partial(second_kernel, chunks),
        out_shape=pltpu.VMEM(sigma.shape, F32),
        in_specs=[SMEM, HBM, HBM, VMEM],
        out_specs=VMEM,
        scratch_shapes=[held, held, pltpu.SemaphoreType.DMA((2, chunks * CHUNK))],
        cost_estimate=pl.CostEstimate(
            flops=chunks * 1_000_000_000, bytes_accessed=chunks << 21, transcendentals=0
        ),
        compiler_params=PARAMS,
        name="second",
    )(start, far(green), far(inject), near_core(sigma))


def pack_kernel(home_ref, away_ref, out_ref):
    for r in range(home_ref.shape[0]):
        out_ref[r, 0] = home_ref[r]
        out_ref[r, 1] = away_ref[r]


def pack(home, away):
    count, size, _ = home.shape
    return pl.pallas_call(
        pack_kernel,
        out_shape=pltpu.VMEM((count, 2, size, size), F32),
        in_specs=[VMEM] * 2,
        out_specs=VMEM,
        cost_estimate=pl.CostEstimate(flops=0, bytes_accessed=1 << 20, transcendentals=0),
        compiler_params=PARAMS,
        name="pack",
    )(near_core(home), near_core(away))


def store_kernel(half_ref, away_ref, home_ref, both_ref, out_ref, sems):
    slices = sems.shape[1]
    group = slices // 2
    copies = []
    for index in range(slices):
        at = lax.rem(group * (1 - half_ref[0]) + index, slices)
        chunk, j = divmod(index % group, CHUNK)
        for part in range(2):
            unit = 2 * j + part
            there = index < group
            if chunk:
                source = both_ref.at[unit, int(there)]
            else:
                source = (away_ref if there else home_ref).at[unit]
            copies.append(pltpu.make_async_copy(source, out_ref.at[0, part, at], sems.at[part, index]))
    for copy in copies:
        copy.start()
    for copy in copies:
        copy.wait()


def store(half, away, home, both, shape):
    return pl.pallas_call(
        store_kernel,
        out_shape=pltpu.HBM(shape, F32),
        in_specs=[SMEM, VMEM, VMEM, VMEM],
        out_specs=HBM,
        scratch_shapes=[pltpu.SemaphoreType.DMA((2, shape[2]))],
        cost_estimate=pl.CostEstimate(flops=0, bytes_accessed=4 << 20, transcendentals=0),
        compiler_params=PARAMS,
        name="store",
    )(half, near_core(away), near_core(home), near_core(both))


def cut_kernel(both_ref, *outs):
    for chunk in range(2):
        for r in range(both_ref.shape[0]):
            outs[chunk][r] = both_ref[r, chunk]


def cut(both):
    count, _, size, _ = both.shape
    return pl.pallas_call(
        cut_kernel,
        out_shape=(pltpu.VMEM((count, size, size), F32),) * 2,
        in_specs=[VMEM],
        out_specs=(VMEM,) * 2,
        cost_estimate=pl.CostEstimate(flops=0, bytes_accessed=1 << 20, transcendentals=0),
        compiler_params=PARAMS,
        name="cut",
    )(near_core(both))


def couple_targets(window, shift_ref, weight_ref, matrix_ref, count, write):
    size = window.shape[-1]
    right = []
    left_high, left_low = [], []
    for mode in range(2):
        shift = shift_ref[mode]
        summed = jnp.concatenate(
            [
                weight_ref[mode, 0] * window[count + t + shift]
                + weight_ref[mode, 1] * window[count + t - shift]
                for t in range(count)
            ],
            axis=0,
        )
        matrix_high, matrix_low = split(matrix_ref[mode])
        left_high.append(matrix_high)
        left_low.append(matrix_low)
        high, low = split(summed)
        right.append(
            dot_t(
                jnp.concatenate([high, low], axis=1),
                jnp.concatenate([matrix_high, matrix_high], axis=1),
            )
            + dot_t(high, matrix_low)
        )
    both_high = jnp.concatenate(left_high, axis=1)
    both_low = jnp.concatenate(left_low, axis=1)
    for t in range(0, count, 2):
        stacked = jnp.concatenate(
            [
                jnp.concatenate([right[m][(t + i) * size : (t + i + 1) * size] for i in range(2)], axis=1)
                for m in range(2)
            ],
            axis=0,
        )
        high, low = split(stacked)
        out = dot(both_high, high) + (dot(both_low, high) + dot(both_high, low))
        for i in range(2):
            write(t + i, out[:, i * size : (i + 1) * size])


def couple_kernel(half_ref, shift_ref, weight_ref, matrix_ref, low_ref, mid_ref, high_ref, out_ref, window):
    count = mid_ref.shape[0]
    half = half_ref[0]

    for r in range(count):
        window[2 * count * half + r] = low_ref[r]
        window[count + r] = mid_ref[r]
        window[2 * count * (1 - half) + r] = high_ref[r]

    def write(index, value):
        out_ref[index] = value

    couple_targets(window, shift_ref, weight_ref, matrix_ref, count, write)


def couple(half, shift, weight, matrices, low, mid, high):
    count, size = mid.shape[0], mid.shape[-1]
    vectors = [near_core(x) for x in (low, mid, high)]
    return pl.pallas_call(
        couple_kernel,
        out_shape=pltpu.VMEM(mid.shape, F32),
        in_specs=[SMEM] * 3 + [VMEM] * (1 + len(vectors)),
        out_specs=VMEM,
        scratch_shapes=[pltpu.VMEM((3 * count, size, size), F32)],
        cost_estimate=pl.CostEstimate(flops=1_000_000_000, bytes_accessed=2 << 20, transcendentals=0),
        compiler_params=PARAMS,
        name="couple",
    )(half, shift, weight, matrices, *vectors)


def last_kernel(half_ref, near_ref, away0_ref, home0_ref, away1_ref, home1_ref, out_ref, held, mixed, sems):
    slices = held.shape[0]
    group = slices // 2
    half = half_ref[0]
    for index in range(slices):
        at = lax.rem(group * (1 - half) + index, slices)
        chunk, j = divmod(index % group, CHUNK)
        for part in range(2):
            refs = (away0_ref, away1_ref) if index < group else (home0_ref, home1_ref)
            held[at, part] = refs[chunk][2 * j + part]

    def store(s):
        return pltpu.make_async_copy(mixed.at[s], out_ref.at[0, :, s], sems.at[s])

    for s in range(slices):
        mixed[s] = held[s] + 0.5 * held[near_ref[s]]
        store(s).start()
    for s in range(slices):
        store(s).wait()


def last(half, near, pieces, shape):
    _, _, slices, size, _ = shape
    held = pltpu.VMEM((slices, 2, size, size), F32)
    return pl.pallas_call(
        last_kernel,
        out_shape=pltpu.HBM(shape, F32),
        in_specs=[SMEM, SMEM] + [VMEM] * 4,
        out_specs=HBM,
        scratch_shapes=[held, held, pltpu.SemaphoreType.DMA((slices,))],
        compiler_params=PARAMS,
        name="last",
    )(half, near, *map(near_core, pieces))


def local(windows, retarded, injection, coupling_matrices, phonon_weight, phonon_shift, slice_neighbour):
    half = (lax.axis_index("inner") // 8).astype(jnp.int32).reshape(1)
    groups = [list(range(8)), list(range(8, 16))]
    across = [(i, (i + 8) % 16) for i in range(16)]

    def neighbours(sign):
        pairs = []
        for w in range(windows):
            for i in range(16):
                to = w + sign * (1 if i >= 8 else -1)
                if 0 <= to < windows:
                    pairs.append((w * 16 + i, to * 16 + i))
        return pairs

    home_pairs, away_pairs = neighbours(1), neighbours(-1)

    def exchange(x):
        return lax.ppermute(x, "inner", across)

    def spread(x):
        return lax.all_to_all(x, "inner", 0, 0, axis_index_groups=groups, tiled=True)

    def halo(x, pairs):
        return lax.ppermute(x, BOTH, pairs)

    common = (half, phonon_shift, phonon_weight, coupling_matrices)
    green, inject = retarded, injection
    far_half = 1 - half
    out, home, both = first(half, slice_neighbour, green, inject)
    for i in range(2):
        got = exchange(out)
        here1, send = cut(spread(both))
        away1 = exchange(send)
        here0 = spread(home)
        halo0 = halo(here0, home_pairs)
        halo1 = halo(here1, home_pairs)
        away0 = spread(got)
        back0 = spread(couple(*common, here0, away0, halo0))
        back0 = exchange(back0)
        back1 = couple(*common, here1, away1, halo1)
        back1 = exchange(back1 if i == 0 else spread(back1))
        far0 = halo(away0, away_pairs)
        far1 = halo(away1, away_pairs)
        here0 = spread(couple(*common, far0, here0, away0))
        here1 = couple(*common, far1, here1, away1)
        if i == 0:
            both = spread(pack(here1, back1))
            starts = jnp.concatenate([half, far_half]) * 8 + CHUNK
            home = second(8 * half, green, inject, here0)
            out = second(8 * far_half, green, inject, back0)
            both = second(starts, green, inject, both)
            lesser = store(half, out, home, both, injection.shape)
    here1 = spread(here1)
    sigma = last(half, slice_neighbour, (back0, here0, back1, here1), injection.shape)
    return lesser, sigma


def solution(mesh):
    blocks = P(BOTH, None, None, None, None)
    return jax.shard_map(
        functools.partial(local, mesh.shape["egrp"]),
        mesh=mesh,
        in_specs=(blocks, blocks, P(), P(), P(), P()),
        out_specs=(blocks, blocks),
        check_vma=False,
    )
```
